32 devices in a mesh: grp: 2 (over x), lon: 16 (over z, y, core), lat: 1.
Axes of the slice: x: 2, y: 2, z: 4, core: 2. Of those that a mesh axis runs over, the one named last changes fastest.
Arguments:
- tokens: bfloat16 [4, 8, 128, 1536], P('grp', 'lat', 'lon'), parts along dimension 0, may hold values from -6 to 6
- land: int32 [16, 128], P(('grp', 'lat'), 'lon'), parts along dimension 0, may hold values 0 or 1
- surface: float32 [2, 1536], replicated, may hold values from -4 to 4
- gain: float32 [1536], replicated, may hold values from 0.25 to 1.75
- weights: bfloat16 [1536, 3072], P('lon'), may hold values from -0.15625 to 0.15625
- shifts: int32 [2, 2], replicated, may hold values from 1 to 7, as said below
- index_table: int32 [64, 64], replicated, may hold values from 0 to 224
- bias_table: float32 [2, 225, 12], P('lat'), as said below
- cotangent: bfloat16 [4, 8, 128, 1536], P('grp', 'lat', 'lon'), parts along dimension 0, may hold values from -6 to 6
Outputs:
- output: bfloat16 [4, 8, 128, 1536], P('grp', 'lat', 'lon'), parts along dimension 0
- grad_tokens: bfloat16 [4, 8, 128, 1536], P('grp', 'lat', 'lon'), parts along dimension 0
- grad_weights: float32 [3072, 3072], P(('grp', 'lon')), parts along dimension 0
The draws below stay inside these ranges and needn't reach their ends.
There are 2 independent parts, one for each index of `grp`. The reference program is written for one: setup_inputs(seed, part) draws one part's arguments, and reference() takes and returns one part's arrays. A program takes and returns all parts, laid end to end along the dimension named above; an argument that names none is the same for every part. Nothing has to cross between parts.
Inputs may be any that keep to these rules, and one draw needn't show every extreme that they name: `shifts`: row l holds level l's offsets along latitude and longitude; taken together the entries include 1 and 7. `bias_table`: every entry is finite.
All inputs are finite; a program needn't handle non-finite values. No bound on the sum of `land` on one device may be relied on, other than what follows from the above.
Results may differ from the reference program's by a relative error of at most 0.023.
Values may be sent and summed in bfloat16 or wider, within the bound.
A program may use at most 128 MiB of HBM per device.

```python
import math
import jax
import jax.numpy as jnp
from jax import lax

D = 1536
HEADS = 12
HDIM = 64
WIN = 8
LVL = 2
CLON = 8
HD = 768
NREL = 225
NLAT = 8
NLON = 128
BANDS = 2
N_LON = 16
N_LAT = 1


def draw_shifts(key, part):
    count = 2 * LVL
    key_vals, key_order = jax.random.split(jax.random.fold_in(key, 5), 2)
    values = jax.random.randint(key_vals, (count,), 1, WIN)
    order = jax.random.permutation(key_order, count)
    values = values.at[order[0]].set(1)
    values = values.at[order[1]].set(WIN - 1)
    return values.reshape(LVL, 2).astype(jnp.int32)


def draw_bias_table(key, part):
    shape = (BANDS, NREL, HEADS)
    key_base = jax.random.fold_in(jax.random.fold_in(key, 11), 0)
    return jnp.clip(jax.random.normal(key_base, shape, jnp.float32), -4.0, 4.0)


def place_ends(drawn, stream_key, low, high):
    place = [jax.random.randint(jax.random.fold_in(stream_key, axis), (), 0, length) for axis, length in enumerate(drawn.shape)]
    widest = drawn.shape.index(max(drawn.shape))
    next_to = place[:widest] + [(place[widest] + 1) % drawn.shape[widest]] + place[widest + 1:]
    return drawn.at[tuple(place)].set(low).at[tuple(next_to)].set(high)


def block_levels(stream_key, extent, cuts, least, largest):
    level, own = 1.0, jax.random.fold_in(stream_key, 6)
    for dim, shards_of in cuts:
        draws = jnp.exp(jax.random.uniform(jax.random.fold_in(own, dim), (shards_of,), jnp.float32, least / len(cuts), largest / len(cuts)))
        level = level * jnp.repeat(draws, extent[dim] // shards_of).reshape([-1 if axis == dim else 1 for axis in range(len(extent))])
    return level


def normal_values(stream_key, shape, deviation, bound, cuts=(), held_as=jnp.bfloat16):
    entries = deviation * jax.random.normal(stream_key, shape, jnp.float32)
    if cuts:
        entries = entries * block_levels(stream_key, shape, cuts, -0.22, 0.18)
    return jnp.clip(entries, -bound, bound).astype(held_as)


def setup_inputs(seed: int = 0, part: int = 0) -> dict:
    key_list = jax.random.split(jax.random.key(seed), 10)
    part_splits = jax.random.split(jax.random.fold_in(key_list[9], part), 10)
    return {
        "tokens": normal_values(part_splits[0], (LVL, NLAT, NLON, D), 1.0, 6.0, ((2, 16),)),
        "land": place_ends((jax.random.randint(part_splits[1], (NLAT, NLON), 0, 10) < 3).astype(jnp.int32), jax.random.fold_in(part_splits[1], 1), 0, 1),
        "surface": normal_values(key_list[2], (2, D), 0.7, 4.0, (), jnp.float32),
        "gain": jnp.clip(1.0 + 0.15 * jax.random.normal(key_list[3], (D,), jnp.float32), 0.25, 1.75),
        "weights": normal_values(key_list[4], (D, 4 * HD), D ** -0.5, 0.15625, ((0, 16),)),
        "shifts": draw_shifts(jax.random.fold_in(key_list[9], 71), part),
        "index_table": place_ends(jax.random.randint(key_list[6], (WIN * WIN, WIN * WIN), 0, NREL), jax.random.fold_in(key_list[6], 1), 0, NREL - 1).astype(jnp.int32),
        "bias_table": draw_bias_table(jax.random.fold_in(key_list[9], 71), part),
        "cotangent": normal_values(part_splits[8], (LVL, NLAT, NLON, D), 1.0, 6.0, ((2, 16),)),
    }


epsilon = 1e-05

def rounded(values):
    return lax.optimization_barrier(values.astype(jnp.bfloat16)).astype(jnp.float32)

def normalize(stream, gain):
    values = stream.astype(jnp.float32)
    center = values - lax.optimization_barrier(jnp.mean(values, axis=-1, keepdims=True))
    spread = lax.rsqrt(lax.optimization_barrier(jnp.mean(center * center, axis=-1, keepdims=True)) + epsilon)
    return (center * spread * gain).astype(jnp.bfloat16)

def normalize_back(stream, gain, grad_normed):
    values = stream.astype(jnp.float32)
    center = values - lax.optimization_barrier(jnp.mean(values, axis=-1, keepdims=True))
    spread = lax.rsqrt(lax.optimization_barrier(jnp.mean(center * center, axis=-1, keepdims=True)) + epsilon)
    scaled = center * spread
    upstream = grad_normed.astype(jnp.float32) * gain
    return spread * (upstream - lax.optimization_barrier(jnp.mean(upstream, axis=-1, keepdims=True)) - scaled * lax.optimization_barrier(jnp.mean(upstream * scaled, axis=-1, keepdims=True)))

def roll_grid(field, shifts, sign):
    planes = []
    for level in range(field.shape[0]):
        planes.append(jnp.roll(field[level], (-sign * shifts[level, 0], -sign * shifts[level, 1]), axis=(0, 1)))
    return jnp.stack(planes)

def reference(tokens, land, surface, gain, weights, shifts, index_table, bias_table, cotangent):
    width = HEADS * HDIM
    area = WIN * WIN
    columns = NLON // WIN
    scale = 1.0 / math.sqrt(HDIM)
    surface_term = jnp.where(land[None, :, :, None] == 1, surface[1], surface[0])
    stream = (tokens.astype(jnp.float32) + surface_term).astype(jnp.bfloat16)
    normed = normalize(stream, gain)
    rolled = roll_grid(normed, shifts, 1)
    rolled_cot = roll_grid(cotangent, shifts, 1)
    w_qkv = weights[:, :3 * width]
    w_out = weights[:, 3 * width:]
    qkv = jnp.dot(rolled.reshape(-1, D), w_qkv, preferred_element_type=jnp.float32)
    view = rounded(qkv).reshape(LVL, N_LAT, WIN, columns, WIN, 3, HEADS, HDIM)
    query = view[:, :, :, :, :, 0]
    keys = view[:, :, :, :, :, 1]
    values = view[:, :, :, :, :, 2]
    six = (LVL, N_LAT, columns, HEADS, area, area)
    seven = (LVL, N_LAT, columns, HEADS, WIN, WIN, WIN, WIN)
    scores = jnp.einsum('liawbhd,licwehd->liwhabce', query, keys).reshape(six)
    onehot = (index_table[:, :, None] == jnp.arange(NREL, dtype=jnp.int32)).astype(jnp.float32)
    bias = jnp.einsum('qkr,srh->shqk', onehot, bias_table, precision=lax.Precision.HIGHEST)
    bias = bias.reshape(N_LAT, LVL, HEADS, area, area).transpose(1, 0, 2, 3, 4)
    rows = jnp.arange(NLAT, dtype=jnp.int32)
    group = rows[None, :] >= (NLAT - shifts[:, 0])[:, None]
    group = jnp.repeat(group.reshape(LVL, N_LAT, WIN), WIN, axis=2)
    allowed = group[:, :, :, None] == group[:, :, None, :]
    scores = scores * scale + bias[:, :, None]
    scores = jnp.where(allowed[:, :, None, None], scores, -1e+30)
    top = lax.optimization_barrier(jnp.max(scores, axis=-1, keepdims=True))
    expo = jnp.exp(scores - top)
    probs = expo / lax.optimization_barrier(jnp.sum(expo, axis=-1, keepdims=True))
    probs_b = rounded(probs).reshape(seven)
    mixed = jnp.einsum('liwhabce,licwehd->liawbhd', probs_b, values).astype(jnp.bfloat16)
    mixed_flat = mixed.reshape(-1, width)
    attended = jnp.dot(mixed_flat, w_out.T, preferred_element_type=jnp.float32).astype(jnp.bfloat16)
    attended = attended.reshape(LVL, NLAT, NLON, D)
    output = (stream.astype(jnp.float32) + roll_grid(attended, shifts, -1).astype(jnp.float32)).astype(jnp.bfloat16)
    cot_flat = rolled_cot.reshape(-1, D)
    grad_mixed = jnp.dot(cot_flat, w_out, preferred_element_type=jnp.float32)
    grad_mixed = rounded(grad_mixed).reshape(LVL, N_LAT, WIN, columns, WIN, HEADS, HDIM)
    grad_probs = jnp.einsum('liawbhd,licwehd->liwhabce', grad_mixed, values).reshape(six)
    grad_values = jnp.einsum('liwhabce,liawbhd->licwehd', probs_b, grad_mixed).astype(jnp.bfloat16)
    grad_scores = probs * (grad_probs - lax.optimization_barrier(jnp.sum(probs * grad_probs, axis=-1, keepdims=True)))
    grad_scores = rounded(grad_scores * scale).reshape(seven)
    grad_query = jnp.einsum('liwhabce,licwehd->liawbhd', grad_scores, keys).astype(jnp.bfloat16)
    grad_keys = jnp.einsum('liwhabce,liawbhd->licwehd', grad_scores, query).astype(jnp.bfloat16)
    grad_qkv = jnp.stack([grad_query, grad_keys, grad_values], axis=5).reshape(-1, 3 * width)
    grad_normed = jnp.dot(grad_qkv, w_qkv.T, preferred_element_type=jnp.float32).astype(jnp.bfloat16)
    grad_normed = roll_grid(grad_normed.reshape(LVL, NLAT, NLON, D), shifts, -1)
    grad_stream = normalize_back(stream, gain, grad_normed)
    grad_tokens = (cotangent.astype(jnp.float32) + grad_stream).astype(jnp.bfloat16)

    def split_tiles(field):
        return jnp.moveaxis(field.reshape(LVL, N_LAT, WIN, N_LON, CLON, -1), 3, 0)
    in_tiles = split_tiles(rolled)
    cot_tiles = split_tiles(rolled_cot)
    qkv_tiles = split_tiles(grad_qkv.reshape(LVL, NLAT, NLON, 3 * width))
    mixed_tiles = split_tiles(mixed_flat.reshape(LVL, NLAT, NLON, width))

    def add_tile(total, pieces):
        in_tile, cot_tile, qkv_tile, mixed_tile = pieces
        first = jnp.einsum('liacx,liacy->ixy', in_tile.astype(jnp.float32), qkv_tile.astype(jnp.float32))
        second = jnp.einsum('liacx,liacy->ixy', cot_tile.astype(jnp.float32), mixed_tile.astype(jnp.float32))
        part = rounded(jnp.concatenate([first, second], axis=2))
        return (total + lax.optimization_barrier(jnp.sum(part, axis=0)), None)
    total, _ = lax.scan(add_tile, jnp.zeros((D, 4 * width), jnp.float32), (in_tiles, cot_tiles, qkv_tiles, mixed_tiles))
    grad_weights = total * (1.0 / math.sqrt(LVL * NLAT * NLON))
    return (output, grad_tokens, grad_weights)
```

```python
import functools
import math

import jax
import jax.numpy as jnp
from jax import lax
from jax.experimental import pallas as pl
from jax.experimental.pallas import tpu as pltpu
from jax.sharding import PartitionSpec as P

epsilon = 1e-05
f32 = jnp.float32
bf16 = jnp.bfloat16
VMEM = pl.BlockSpec(memory_space=pltpu.VMEM)


def passed_along(shard, axis, by):
    count = lax.axis_size(axis)
    return lax.ppermute(shard, axis, [(i, (i + by) % count) for i in range(count)])


def dot(a, b, dims):
    return lax.dot_general(a, b, ((dims[0], dims[1]), ((), ())), preferred_element_type=f32)


def normalize(stream, gain):
    values = stream.astype(f32)
    center = values - jnp.mean(values, axis=-1, keepdims=True)
    spread = lax.rsqrt(jnp.mean(center * center, axis=-1, keepdims=True) + epsilon)
    return (center * spread * gain).astype(bf16)


def normalize_back(stream, gain, grad_normed):
    values = stream.astype(f32)
    center = values - jnp.mean(values, axis=-1, keepdims=True)
    spread = lax.rsqrt(jnp.mean(center * center, axis=-1, keepdims=True) + epsilon)
    scaled = center * spread
    upstream = grad_normed.astype(f32) * gain
    return spread * (
        upstream
        - jnp.mean(upstream, axis=-1, keepdims=True)
        - scaled * jnp.mean(upstream * scaled, axis=-1, keepdims=True)
    )


def take_levels(field, starts, axis, length):

    def one_level(plane, start):
        return lax.dynamic_slice_in_dim(plane, start, length, axis - 1)

    return jax.vmap(one_level, in_axes=(1, 0), out_axes=1)(field, starts)


def attend_kernel(width, p_own, p_east, mine, east, w, bias, rolled, qkvm, grads, dw, proj):
    tokens, model = rolled.shape[1:]
    for part in range(2):
        def roll_tile(t, _):
            cols = pl.ds(pl.multiple_of(t * 512, 512), 512)
            moved = dot(p_own[...], mine[part, :, cols], ((1,), (0,)))
            moved += dot(p_east[...], east[part, :, cols], ((1,), (0,)))
            rolled[part, :, cols] = moved.astype(bf16)
            return 0
        lax.fori_loop(0, model // 512, roll_tile, 0)

    def proj_tile(src):
        def body(t, _):
            cols = pl.ds(pl.multiple_of(t * 256, 256), 256)
            proj[:, cols] = dot(rolled[src], w[:, cols], ((1,), (0,))).astype(bf16)
            return 0
        return body

    lax.fori_loop(0, 3 * width // 256, proj_tile(0), 0)
    lax.fori_loop(3 * width // 256, 4 * width // 256, proj_tile(1), 0)

    left = lax.broadcasted_iota(jnp.int32, (tokens, 128), 1) < 64
    scale = 0.125

    def pair(j, _):
        def cols(block):
            return pl.ds(pl.multiple_of(block * width + j * 128, 128), 128)
        q, k, v, g = (proj[:, cols(b)] for b in range(4))
        outs = []
        for half in range(2):
            keep = left if half == 0 else jnp.logical_not(left)
            zero = jnp.zeros_like(q)
            s = dot(jnp.where(keep, q, zero), k, ((1,), (1,))) * scale + bias[2 * j + half]
            top = jnp.max(s, axis=-1, keepdims=True)
            expo = jnp.exp(s - top)
            probs = expo / jnp.sum(expo, axis=-1, keepdims=True)
            probs_b = probs.astype(bf16)
            mixed = dot(probs_b, v, ((1,), (0,)))
            grad_probs = dot(jnp.where(keep, g, zero), v, ((1,), (1,)))
            grad_v = dot(probs_b, g, ((0,), (0,)))
            inner = jnp.sum(probs * grad_probs, axis=-1, keepdims=True)
            gs = (probs * (grad_probs - inner) * scale).astype(bf16)
            outs.append((mixed, dot(gs, k, ((1,), (0,))), dot(gs, q, ((0,), (0,))), grad_v))
        mixed, grad_q, grad_k, grad_v = (jnp.where(left, a, b).astype(bf16) for a, b in zip(*outs))
        grads[:, cols(0)] = grad_q
        grads[:, cols(1)] = grad_k
        grads[:, cols(2)] = grad_v
        grads[:, cols(3)] = mixed
        return 0

    lax.fori_loop(0, width // 128, pair, 0)

    def weight_tile(t, _):
        rows = pl.ds(pl.multiple_of(t * 128, 128), 128)
        first = dot(rolled[0, :, rows], grads[:, : 3 * width], ((0,), (0,)))
        dw[rows, : 3 * width] = first.astype(bf16)
        second = dot(rolled[1, :, rows], grads[:, 3 * width :], ((0,), (0,)))
        dw[rows, 3 * width :] = second.astype(bf16)
        return 0

    lax.fori_loop(0, model // 128, weight_tile, 0)


def project_kernel(width, p_own, p_east, grads, w, keep, send):
    model = w.shape[0]

    def body(t, _):
        rows = pl.ds(pl.multiple_of(t * 256, 256), 256)
        attended = dot(grads[:, 3 * width :], w[rows, 3 * width :], ((1,), (1,))).astype(bf16)
        grad_normed = dot(grads[:, : 3 * width], w[rows, : 3 * width], ((1,), (1,))).astype(bf16)
        for part, field in enumerate((attended, grad_normed)):
            keep[part, :, rows] = dot(p_own[...], field, ((0,), (0,))).astype(bf16)
            send[part, :, rows] = dot(p_east[...], field, ((0,), (0,))).astype(bf16)
        return 0

    lax.fori_loop(0, model // 256, body, 0)


def on_device(tokens, land, surface, gain, weights, shifts, index_table, bias_table, cotangent):
    levels, tile_rows, tile_cols, model = tokens.shape
    heads = bias_table.shape[2]
    entries = bias_table.shape[1]
    width = weights.shape[1] // 4
    count = levels * tile_rows * tile_cols
    area = tile_rows * tile_rows
    lats = lax.axis_size("lat")
    w = lax.all_gather(weights, "lon", axis=0, tiled=True)

    surface_term = jnp.where(land[None, :, :, None] == 1, surface[1], surface[0])
    stream = (tokens.astype(f32) + surface_term).astype(bf16)
    fields = jnp.stack([normalize(stream, gain), cotangent])
    row_shift = shifts[:, 0]
    if lats > 1:
        below = passed_along(fields, "lat", -1)
        both = jnp.concatenate([fields, below], axis=2)
        fields = jax.vmap(lambda f: take_levels(f[None], row_shift, 2, tile_rows)[0])(both)
        row_shift = jnp.zeros_like(row_shift)
    mine = fields.reshape(2, count, model)
    east = passed_along(mine, "lon", -1)

    cell = jnp.arange(count, dtype=jnp.int32)
    lev, row, col = cell // (tile_rows * tile_cols), cell // tile_cols % tile_rows, cell % tile_cols
    from_row = (row + row_shift[lev]) % tile_rows
    from_col = col + shifts[lev, 1]
    source = lev * tile_rows * tile_cols + from_row * tile_cols + from_col % tile_cols
    hit = source[:, None] == cell[None, :]
    inside = (from_col < tile_cols)[:, None]
    p_own = jnp.where(hit & inside, 1.0, 0.0).astype(bf16)
    p_east = jnp.where(hit & ~inside, 1.0, 0.0).astype(bf16)

    onehot = (index_table[:, :, None] == jnp.arange(entries, dtype=jnp.int32)).astype(f32)
    bias = jnp.einsum("qkr,lrh->hlqk", onehot, bias_table, precision=lax.Precision.HIGHEST)
    total_rows = tile_rows * lats
    row_number = lax.axis_index("lat") * tile_rows + jnp.arange(tile_rows, dtype=jnp.int32)
    group = row_number[None, :] >= (total_rows - shifts[:, 0])[:, None]
    group = jnp.repeat(group, tile_rows, axis=1)
    allowed = group[:, :, None] == group[:, None, :]
    bias = jnp.where(allowed[None], bias, -1e30)
    other = jnp.full((heads, area, area), -jnp.inf, f32)
    bias = jnp.concatenate(
        [jnp.concatenate([bias[:, 0], other], axis=2), jnp.concatenate([other, bias[:, 1]], axis=2)],
        axis=1,
    )

    params = pltpu.CompilerParams(vmem_limit_bytes=56 * 2**20)
    grads, dw = pl.pallas_call(
        lambda a, b, c, d, e, f, g, h, r, p: attend_kernel(width, a, b, c, d, e, f, r, None, g, h, p),
        name="attend",
        out_shape=(
            jax.ShapeDtypeStruct((count, 4 * width), bf16),
            jax.ShapeDtypeStruct((model, 4 * width), bf16),
        ),
        in_specs=[VMEM] * 6,
        out_specs=(VMEM, VMEM),
        scratch_shapes=[pltpu.VMEM((2, count, model), bf16), pltpu.VMEM((count, 4 * width), bf16)],
        compiler_params=params,
        cost_estimate=pl.CostEstimate(flops=3 * 10**9, bytes_accessed=24 * 10**6, transcendentals=200000),
    )(p_own, p_east, mine, east, w, bias)
    summed = lax.psum_scatter(dw, "lon", scatter_dimension=0, tiled=True)
    keep, send = pl.pallas_call(
        functools.partial(project_kernel, width),
        name="project",
        out_shape=(jax.ShapeDtypeStruct((2, count, model), bf16),) * 2,
        in_specs=[VMEM] * 4,
        out_specs=(VMEM, VMEM),
        compiler_params=params,
        cost_estimate=pl.CostEstimate(flops=2 * 10**9, bytes_accessed=13 * 10**6, transcendentals=0),
    )(p_own, p_east, grads, w)
    west = passed_along(send, "lon", 1)
    back = (keep.astype(f32) + west.astype(f32)).astype(bf16)
    back = back.reshape(2, levels, tile_rows, tile_cols, model)
    if lats > 1:
        above = passed_along(back, "lat", 1)
        both = jnp.concatenate([above, back], axis=2)
        starts = tile_rows - shifts[:, 0]
        back = jax.vmap(lambda f: take_levels(f[None], starts, 2, tile_rows)[0])(both)
    output = (stream.astype(f32) + back[0].astype(f32)).astype(bf16)
    grad_stream = normalize_back(stream, gain, back[1])
    grad_tokens = (cotangent.astype(f32) + grad_stream).astype(bf16)
    summed = lax.psum(summed, "lat").astype(f32)
    token_count = count * lats * lax.axis_size("lon")
    grad_weights = summed * (1.0 / math.sqrt(token_count))
    return (output, grad_tokens, grad_weights)


def solution(mesh):
    return jax.shard_map(
        on_device,
        mesh=mesh,
        in_specs=(
            P("grp", "lat", "lon", None),
            P(("grp", "lat"), "lon"),
            P(),
            P(),
            P("lon", None),
            P(),
            P(),
            P("lat", None, None),
            P("grp", "lat", "lon", None),
        ),
        out_specs=(
            P("grp", "lat", "lon", None),
            P("grp", "lat", "lon", None),
            P(("grp", "lon"), None),
        ),
        check_vma=False,
    )
```

```python
import functools
import math

import jax
import jax.numpy as jnp
from jax import lax
from jax.experimental import pallas as pl
from jax.experimental.pallas import tpu as pltpu
from jax.sharding import PartitionSpec as P

epsilon = 1e-05
f32 = jnp.float32
bf16 = jnp.bfloat16
MESH = pl.DeviceIdType.MESH
ANY = pl.BlockSpec(memory_space=pl.ANY)
VMEM = pl.BlockSpec(memory_space=pltpu.VMEM)


def passed_along(shard, axis, by):
    count = lax.axis_size(axis)
    return lax.ppermute(shard, axis, [(i, (i + by) % count) for i in range(count)])


def dot(a, b, dims):
    return lax.dot_general(a, b, ((dims[0], dims[1]), ((), ())), preferred_element_type=f32)


def normalize(stream, gain):
    values = stream.astype(f32)
    center = values - jnp.mean(values, axis=-1, keepdims=True)
    spread = lax.rsqrt(jnp.mean(center * center, axis=-1, keepdims=True) + epsilon)
    return (center * spread * gain).astype(bf16)


def normalize_back(stream, gain, grad_normed):
    values = stream.astype(f32)
    center = values - jnp.mean(values, axis=-1, keepdims=True)
    spread = lax.rsqrt(jnp.mean(center * center, axis=-1, keepdims=True) + epsilon)
    scaled = center * spread
    upstream = grad_normed.astype(f32) * gain
    return spread * (
        upstream
        - jnp.mean(upstream, axis=-1, keepdims=True)
        - scaled * jnp.mean(upstream * scaled, axis=-1, keepdims=True)
    )


def take_levels(field, starts, axis, length):

    def one_level(plane, start):
        return lax.dynamic_slice_in_dim(plane, start, length, axis - 1)

    return jax.vmap(one_level, in_axes=(1, 0), out_axes=1)(field, starts)


def attend_kernel(width, p_own, p_east, mine, east, w, bias, grads, rolled_t, rolled, proj):
    tokens, model = rolled.shape[1:]
    for part in range(2):
        def roll_tile(t, _):
            cols = pl.ds(pl.multiple_of(t * 512, 512), 512)
            moved = dot(p_own[...], mine[part, :, cols], ((1,), (0,)))
            moved += dot(p_east[...], east[part, :, cols], ((1,), (0,)))
            rolled[part, :, cols] = moved.astype(bf16)
            rolled_t[part, cols, :] = moved.T.astype(bf16)
            return 0
        lax.fori_loop(0, model // 512, roll_tile, 0)

    def proj_tile(src):
        def body(t, _):
            cols = pl.ds(pl.multiple_of(t * 256, 256), 256)
            proj[:, cols] = dot(rolled[src], w[:, cols], ((1,), (0,))).astype(bf16)
            return 0
        return body

    lax.fori_loop(0, 3 * width // 256, proj_tile(0), 0)
    lax.fori_loop(3 * width // 256, 4 * width // 256, proj_tile(1), 0)

    left = lax.broadcasted_iota(jnp.int32, (tokens, 128), 1) < 64
    scale = 0.125

    def pair(j, _):
        def cols(block):
            return pl.ds(pl.multiple_of(block * width + j * 128, 128), 128)
        q, k, v, g = (proj[:, cols(b)] for b in range(4))
        outs = []
        for half in range(2):
            keep = left if half == 0 else jnp.logical_not(left)
            zero = jnp.zeros_like(q)
            s = dot(jnp.where(keep, q, zero), k, ((1,), (1,))) * scale + bias[2 * j + half]
            top = jnp.max(s, axis=-1, keepdims=True)
            expo = jnp.exp(s - top)
            probs = expo / jnp.sum(expo, axis=-1, keepdims=True)
            probs_b = probs.astype(bf16)
            mixed = dot(probs_b, v, ((1,), (0,)))
            grad_probs = dot(jnp.where(keep, g, zero), v, ((1,), (1,)))
            grad_v = dot(probs_b, g, ((0,), (0,)))
            inner = jnp.sum(probs * grad_probs, axis=-1, keepdims=True)
            gs = (probs * (grad_probs - inner) * scale).astype(bf16)
            outs.append((mixed, dot(gs, k, ((1,), (0,))), dot(gs, q, ((0,), (0,))), grad_v))
        mixed, grad_q, grad_k, grad_v = (jnp.where(left, a, b).astype(bf16) for a, b in zip(*outs))
        grads[:, cols(0)] = grad_q
        grads[:, cols(1)] = grad_k
        grads[:, cols(2)] = grad_v
        grads[:, cols(3)] = mixed
        return 0

    lax.fori_loop(0, width // 128, pair, 0)


def where_am_i():
    me = lax.axis_index("lon")
    return me, me // 4, me // 2 % 2, me % 2


def index_of(z, y, c):
    return (z * 2 + y) * 2 + c


def signal(barrier, **where):
    pl.semaphore_signal(barrier, inc=1, device_id=where, device_id_type=MESH)


def line_neighbours(z, last):
    return (z + last) // (last + 1) + (2 * last - z) // (last + 1)


def gather_kernel(n, shard, full, local_sem, send_sem, recv_sem):
    me, z, y, c = where_am_i()
    x = lax.axis_index("grp")
    last = n // 4 - 1
    barrier = pltpu.get_barrier_semaphore()
    signal(barrier, grp=1 - x)
    signal(barrier, lon=index_of(z, y, 1 - c))
    signal(barrier, lon=index_of(z, 1 - y, c))
    pl.when(z > 0)(lambda: signal(barrier, lon=me - 4))
    pl.when(z < last)(lambda: signal(barrier, lon=me + 4))
    pl.semaphore_wait(barrier, 3 + line_neighbours(z, last))

    def whole(j, way, where, src=None):
        return pltpu.make_async_remote_copy(
            full.at[j] if src is None else src, full.at[j],
            send_sem.at[j, way, 0], recv_sem.at[j, 0], device_id=where, device_id_type=MESH)

    def half(j, h, way, where, src=None):
        return pltpu.make_async_remote_copy(
            full.at[j, h] if src is None else src, full.at[j, h],
            send_sem.at[j, way, h], recv_sem.at[j, h], device_id=where, device_id_type=MESH)

    partner = {"lon": index_of(z, y, 1 - c)}
    across = {"lon": index_of(z, 1 - y, c)}
    right, left, peer = {"lon": me + 4}, {"lon": me - 4}, {"grp": 1 - x}

    def spread(j, act, src=None, to_right=True, to_left=True):
        if to_right:
            pl.when(z < last)(lambda: act(whole(j, 0, right, src)))
        if to_left:
            pl.when(z > 0)(lambda: act(whole(j, 1, left, src)))
        act(half(j, x, 2, across, None if src is None else src.at[x]))
        act(whole(j, 3, partner, src))

    def own_column(t, act):
        def from_left():
            act(me - 4 * t, dict(to_left=False))
        def from_right():
            act(me + 4 * t, dict(to_right=False))
        pl.when(z - t >= 0)(from_left)
        pl.when(z + t <= last)(from_right)

    def other_column(t, act):
        base = index_of(z, 1 - y, c)
        if t == 0:
            act(base)
        else:
            pl.when(z - t >= 0)(lambda: act(base - 4 * t))
            pl.when(z + t <= last)(lambda: act(base + 4 * t))

    start = lambda copy: copy.start()
    keep = pltpu.make_async_copy(shard, full.at[me], local_sem)
    spread(me, start, shard)
    keep.start()

    def arrived(j, ways):
        whole(j, 0, right).wait_recv()
        spread(j, start, **ways)

    def across_arrived(j):
        half(j, x, 2, across).wait_recv()
        half(j, x, 4, peer).start()
        half(j, x, 3, partner).start()

    def peer_arrived(j):
        half(j, 1 - x, 4, peer).wait_recv()
        half(j, 1 - x, 3, partner).start()

    for t in range(1, last + 1):
        own_column(t, arrived)
        other_column(t - 1, across_arrived)
        if t > 1:
            other_column(t - 2, peer_arrived)
    other_column(last, across_arrived)
    other_column(last - 1, peer_arrived)
    other_column(last, peer_arrived)

    def partner_block(i, _):
        whole(index_of(i, y, 1 - c), 3, partner).wait_recv()
        half(index_of(i, 1 - y, 1 - c), 0, 3, partner).wait_recv()
        half(index_of(i, 1 - y, 1 - c), 1, 3, partner).wait_recv()
        return 0

    lax.fori_loop(0, last + 1, partner_block, 0)
    keep.wait()
    sent = lambda copy: copy.wait_send()
    spread(me, sent, shard)
    for t in range(1, last + 1):
        own_column(t, lambda j, ways: spread(j, sent, **ways))

    def other_sent(j):
        half(j, x, 4, peer).wait_send()
        half(j, x, 3, partner).wait_send()
        half(j, 1 - x, 3, partner).wait_send()

    for t in range(last + 1):
        other_column(t, other_sent)


def scatter_kernel(width, n, p_own, p_east, grads, rolled_t, w_hbm, back, out,
                   w, mine, theirs, from_core, from_y, from_z, keep, send, west,
                   load_sem, core_s, core_r, y_s, y_r, z_s, z_r, west_s, west_r):
    me, z, y, c = where_am_i()
    model = w.shape[0]
    depth = model // n
    last = n // 4 - 1
    load = pltpu.make_async_copy(w_hbm, w, load_sem)
    load.start()
    ahead = (me + 1) % n
    barrier = pltpu.get_barrier_semaphore()
    signal(barrier, lon=index_of(z, y, 1 - c))
    signal(barrier, lon=index_of(z, 1 - y, c))
    signal(barrier, lon=(me + 2 * c - 1 + n) % n)
    pl.when(z > 0)(lambda: signal(barrier, lon=me - 4))
    pl.when(z < last)(lambda: signal(barrier, lon=me + 4))
    pl.semaphore_wait(barrier, 3 + line_neighbours(z, last))

    def remote(src, dst, ssem, rsem, lon):
        return pltpu.make_async_remote_copy(
            src, dst, ssem, rsem, device_id={"lon": lon}, device_id_type=MESH)

    def core_copy(k):
        return remote(theirs.at[k], from_core.at[k], core_s.at[k], core_r.at[k], index_of(z, y, 1 - c))

    def y_copy(k):
        return remote(mine.at[k], from_y.at[k], y_s.at[k], y_r.at[k], index_of(z, 1 - y, c))

    def z_copy(m, d, way):
        to = me + 4 if way == 0 else me - 4
        return remote(mine.at[4 + m], from_z.at[way, d], z_s.at[way, m], z_r.at[way, d], to)

    def weight_block(j, dst):
        rows = pl.ds(pl.multiple_of(j * depth, depth), depth)
        for part, begin, end in ((0, 0, 3 * width), (1, 3 * width, 4 * width)):
            def chunk(t, _):
                cols = pl.ds(pl.multiple_of(t * 384, 128), 384)
                dst[:, cols] = dot(rolled_t[part, rows, :], grads[:, cols], ((1,), (0,))).astype(bf16)
                return 0
            lax.fori_loop(begin // 384, end // 384, chunk, 0)

    order = [3 - 3 * (z // 2), (2 + 3 * z) % 5, 1 + z % 2, z]

    def add(dst, *others):
        total = dst[...].astype(f32)
        for other in others:
            total += other[...].astype(f32)
        dst[...] = total.astype(bf16)

    def pass_across(k):
        core_copy(k).wait_recv()
        add(mine.at[k], from_core.at[k])
        y_copy(k).start()

    for k in range(8):
        chip = order[k % 4] * 2 + (1 - y if k < 4 else y)
        weight_block(chip * 2 + 1 - c, theirs.at[k])
        core_copy(k).start()
        weight_block(chip * 2 + c, mine.at[k])
        if 1 <= k <= 4:
            pass_across(k - 1)

    load.wait()

    def project(t, _):
        rows = pl.ds(pl.multiple_of(t * 256, 256), 256)
        attended = dot(grads[:, 3 * width :], w[rows, 3 * width :], ((1,), (1,))).astype(bf16)
        grad_normed = dot(grads[:, : 3 * width], w[rows, : 3 * width], ((1,), (1,))).astype(bf16)
        for part, field in enumerate((attended, grad_normed)):
            keep[part, :, rows] = dot(p_own[...], field, ((0,), (0,))).astype(bf16)
            send[part, :, rows] = dot(p_east[...], field, ((0,), (0,))).astype(bf16)
        return 0

    lax.fori_loop(0, model // 256, project, 0)
    west_copy = remote(send, west, west_s, west_r, ahead)
    west_copy.start()

    for m in range(4):
        d = order[m]
        core_copy(4 + m).wait_recv()
        y_copy(m).wait_recv()
        add(mine.at[4 + m], from_core.at[4 + m], from_y.at[m])
        if m < 3:
            def go_right():
                def more():
                    z_copy(m, d, 0).wait_recv()
                    add(mine.at[4 + m], from_z.at[0, d])
                pl.when(z > 0)(more)
                z_copy(m, d, 0).start()

            def go_left():
                def more():
                    z_copy(m, d, 1).wait_recv()
                    add(mine.at[4 + m], from_z.at[1, d])
                pl.when(z < last)(more)
                z_copy(m, d, 1).start()

            pl.when(d > z)(go_right)
            pl.when(d < z)(go_left)

    west_copy.wait_recv()
    back[...] = (keep[...].astype(f32) + west[...].astype(f32)).astype(bf16)
    out[...] = mine[7].astype(f32)

    def final(way):
        z_copy(3, z, way).wait_recv()
        out[...] += from_z[way, z].astype(f32)

    pl.when(z > 0)(lambda: final(0))
    pl.when(z < last)(lambda: final(1))
    west_copy.wait_send()
    for k in range(8):
        core_copy(k).wait_send()
    for k in range(4):
        y_copy(k).wait_send()
    for m in range(3):
        d = order[m]
        pl.when(d > z)(lambda: z_copy(m, d, 0).wait_send())
        pl.when(d < z)(lambda: z_copy(m, d, 1).wait_send())


def on_device(tokens, land, surface, gain, weights, shifts, index_table, bias_table, cotangent):
    levels, tile_rows, tile_cols, model = tokens.shape
    heads = bias_table.shape[2]
    entries = bias_table.shape[1]
    width = weights.shape[1] // 4
    count = levels * tile_rows * tile_cols
    area = tile_rows * tile_rows
    lats = lax.axis_size("lat")
    n = lax.axis_size("lon")
    depth = model // n
    dma = pltpu.SemaphoreType.DMA
    w = pl.pallas_call(
        functools.partial(gather_kernel, n),
        name="gather",
        out_shape=jax.ShapeDtypeStruct((n, 2, depth // 2, 4 * width), bf16),
        in_specs=[VMEM],
        out_specs=ANY,
        scratch_shapes=[dma, dma((n, 5, 2)), dma((n, 2))],
        compiler_params=pltpu.CompilerParams(
            collective_id=0, has_side_effects=True, vmem_limit_bytes=8 * 2**20
        ),
        cost_estimate=pl.CostEstimate(flops=0, bytes_accessed=120 * 10**6, transcendentals=0),
    )(weights.reshape(2, depth // 2, 4 * width))
    w = w.reshape(model, 4 * width)

    surface_term = jnp.where(land[None, :, :, None] == 1, surface[1], surface[0])
    stream = (tokens.astype(f32) + surface_term).astype(bf16)
    fields = jnp.stack([normalize(stream, gain), cotangent])
    row_shift = shifts[:, 0]
    if lats > 1:
        below = passed_along(fields, "lat", -1)
        both = jnp.concatenate([fields, below], axis=2)
        fields = jax.vmap(lambda f: take_levels(f[None], row_shift, 2, tile_rows)[0])(both)
        row_shift = jnp.zeros_like(row_shift)
    mine = fields.reshape(2, count, model)
    east = passed_along(mine, "lon", -1)

    cell = jnp.arange(count, dtype=jnp.int32)
    lev, row, col = cell // (tile_rows * tile_cols), cell // tile_cols % tile_rows, cell % tile_cols
    from_row = (row + row_shift[lev]) % tile_rows
    from_col = col + shifts[lev, 1]
    source = lev * tile_rows * tile_cols + from_row * tile_cols + from_col % tile_cols
    hit = source[:, None] == cell[None, :]
    inside = (from_col < tile_cols)[:, None]
    p_own = jnp.where(hit & inside, 1.0, 0.0).astype(bf16)
    p_east = jnp.where(hit & ~inside, 1.0, 0.0).astype(bf16)

    onehot = (index_table[:, :, None] == jnp.arange(entries, dtype=jnp.int32)).astype(f32)
    bias = jnp.einsum("qkr,lrh->hlqk", onehot, bias_table, precision=lax.Precision.HIGHEST)
    total_rows = tile_rows * lats
    row_number = lax.axis_index("lat") * tile_rows + jnp.arange(tile_rows, dtype=jnp.int32)
    group = row_number[None, :] >= (total_rows - shifts[:, 0])[:, None]
    group = jnp.repeat(group, tile_rows, axis=1)
    allowed = group[:, :, None] == group[:, None, :]
    bias = jnp.where(allowed[None], bias, -1e30)
    other = jnp.full((heads, area, area), -jnp.inf, f32)
    bias = jnp.concatenate(
        [jnp.concatenate([bias[:, 0], other], axis=2), jnp.concatenate([other, bias[:, 1]], axis=2)],
        axis=1,
    )

    params = pltpu.CompilerParams(vmem_limit_bytes=56 * 2**20)
    grads, rolled_t = pl.pallas_call(
        functools.partial(attend_kernel, width),
        name="attend",
        out_shape=(
            jax.ShapeDtypeStruct((count, 4 * width), bf16),
            jax.ShapeDtypeStruct((2, model, count), bf16),
        ),
        in_specs=[VMEM] * 6,
        out_specs=(VMEM, VMEM),
        scratch_shapes=[pltpu.VMEM((2, count, model), bf16), pltpu.VMEM((count, 4 * width), bf16)],
        compiler_params=params,
        cost_estimate=pl.CostEstimate(flops=3 * 10**9, bytes_accessed=15 * 10**6, transcendentals=200000),
    )(p_own, p_east, mine, east, w, bias)
    block = (depth, 4 * width)
    back, summed = pl.pallas_call(
        functools.partial(scatter_kernel, width, n),
        name="scatter",
        out_shape=(
            jax.ShapeDtypeStruct((2, count, model), bf16),
            jax.ShapeDtypeStruct(block, f32),
        ),
        in_specs=[VMEM] * 4 + [ANY],
        out_specs=(VMEM, VMEM),
        scratch_shapes=[
            pltpu.VMEM((model, 4 * width), bf16),
            pltpu.VMEM((8,) + block, bf16),
            pltpu.VMEM((8,) + block, bf16),
            pltpu.VMEM((8,) + block, bf16),
            pltpu.VMEM((4,) + block, bf16),
            pltpu.VMEM((2, 4) + block, bf16),
            pltpu.VMEM((2, count, model), bf16),
            pltpu.VMEM((2, count, model), bf16),
            pltpu.VMEM((2, count, model), bf16),
            dma, dma((8,)), dma((8,)), dma((4,)), dma((4,)), dma((2, 4)), dma((2, 4)), dma, dma,
        ],
        compiler_params=pltpu.CompilerParams(
            collective_id=1, has_side_effects=True, vmem_limit_bytes=60 * 2**20
        ),
        cost_estimate=pl.CostEstimate(flops=3 * 10**9, bytes_accessed=150 * 10**6, transcendentals=0),
    )(p_own, p_east, grads, rolled_t, w)
    back = back.reshape(2, levels, tile_rows, tile_cols, model)
    if lats > 1:
        above = passed_along(back, "lat", 1)
        both = jnp.concatenate([above, back], axis=2)
        starts = tile_rows - shifts[:, 0]
        back = jax.vmap(lambda f: take_levels(f[None], starts, 2, tile_rows)[0])(both)
    output = (stream.astype(f32) + back[0].astype(f32)).astype(bf16)
    grad_stream = normalize_back(stream, gain, back[1])
    grad_tokens = (cotangent.astype(f32) + grad_stream).astype(bf16)
    if lats > 1:
        summed = lax.psum(summed, "lat")
    token_count = count * lats * lax.axis_size("lon")
    grad_weights = summed * (1.0 / math.sqrt(token_count))
    return (output, grad_tokens, grad_weights)


def solution(mesh):
    return jax.shard_map(
        on_device,
        mesh=mesh,
        in_specs=(
            P("grp", "lat", "lon", None),
            P(("grp", "lat"), "lon"),
            P(),
            P(),
            P("lon", None),
            P(),
            P(),
            P("lat", None, None),
            P("grp", "lat", "lon", None),
        ),
        out_specs=(
            P("grp", "lat", "lon", None),
            P("grp", "lat", "lon", None),
            P(("grp", "lon"), None),
        ),
        check_vma=False,
    )
```

```python
import functools
import math

import jax
import jax.numpy as jnp
from jax import lax
from jax.experimental import pallas as pl
from jax.experimental.pallas import tpu as pltpu
from jax.sharding import PartitionSpec as P

epsilon = 1e-05
f32 = jnp.float32
bf16 = jnp.bfloat16
MESH = pl.DeviceIdType.MESH
ANY = pl.BlockSpec(memory_space=pl.ANY)
VMEM = pl.BlockSpec(memory_space=pltpu.VMEM)


def passed_along(shard, axis, by):
    count = lax.axis_size(axis)
    return lax.ppermute(shard, axis, [(i, (i + by) % count) for i in range(count)])


def dot(a, b, dims):
    return lax.dot_general(a, b, ((dims[0], dims[1]), ((), ())), preferred_element_type=f32)


def normalize(stream, gain):
    values = stream.astype(f32)
    center = values - jnp.mean(values, axis=-1, keepdims=True)
    spread = lax.rsqrt(jnp.mean(center * center, axis=-1, keepdims=True) + epsilon)
    return (center * spread * gain).astype(bf16)


def normalize_back(stream, gain, grad_normed):
    values = stream.astype(f32)
    center = values - jnp.mean(values, axis=-1, keepdims=True)
    spread = lax.rsqrt(jnp.mean(center * center, axis=-1, keepdims=True) + epsilon)
    scaled = center * spread
    upstream = grad_normed.astype(f32) * gain
    return spread * (
        upstream
        - jnp.mean(upstream, axis=-1, keepdims=True)
        - scaled * jnp.mean(upstream * scaled, axis=-1, keepdims=True)
    )


def take_levels(field, starts, axis, length):

    def one_level(plane, start):
        return lax.dynamic_slice_in_dim(plane, start, length, axis - 1)

    return jax.vmap(one_level, in_axes=(1, 0), out_axes=1)(field, starts)


def attend_kernel(width, p_own, p_east, mine, east, w, bias, grads, rolled_t, rolled, proj):
    tokens, model = rolled.shape[1:]
    for part in range(2):
        def roll_tile(t, _):
            cols = pl.ds(pl.multiple_of(t * 512, 512), 512)
            moved = dot(p_own[...], mine[part, :, cols], ((1,), (0,)))
            moved += dot(p_east[...], east[part, :, cols], ((1,), (0,)))
            rolled[part, :, cols] = moved.astype(bf16)
            rolled_t[part, cols, :] = moved.T.astype(bf16)
            return 0
        lax.fori_loop(0, model // 512, roll_tile, 0)

    def proj_tile(src):
        def body(t, _):
            cols = pl.ds(pl.multiple_of(t * 256, 256), 256)
            proj[:, cols] = dot(rolled[src], w[:, cols], ((1,), (0,))).astype(bf16)
            return 0
        return body

    lax.fori_loop(0, 3 * width // 256, proj_tile(0), 0)
    lax.fori_loop(3 * width // 256, 4 * width // 256, proj_tile(1), 0)

    left = lax.broadcasted_iota(jnp.int32, (tokens, 128), 1) < 64
    scale = 0.125

    def pair(j, _):
        def cols(block):
            return pl.ds(pl.multiple_of(block * width + j * 128, 128), 128)
        q, k, v, g = (proj[:, cols(b)] for b in range(4))
        outs = []
        for half in range(2):
            keep = left if half == 0 else jnp.logical_not(left)
            zero = jnp.zeros_like(q)
            s = dot(jnp.where(keep, q, zero), k, ((1,), (1,))) * scale + bias[2 * j + half]
            top = jnp.max(s, axis=-1, keepdims=True)
            expo = jnp.exp(s - top)
            probs = expo / jnp.sum(expo, axis=-1, keepdims=True)
            probs_b = probs.astype(bf16)
            mixed = dot(probs_b, v, ((1,), (0,)))
            grad_probs = dot(jnp.where(keep, g, zero), v, ((1,), (1,)))
            grad_v = dot(probs_b, g, ((0,), (0,)))
            inner = jnp.sum(probs * grad_probs, axis=-1, keepdims=True)
            gs = (probs * (grad_probs - inner) * scale).astype(bf16)
            outs.append((mixed, dot(gs, k, ((1,), (0,))), dot(gs, q, ((0,), (0,))), grad_v))
        mixed, grad_q, grad_k, grad_v = (jnp.where(left, a, b).astype(bf16) for a, b in zip(*outs))
        grads[:, cols(0)] = grad_q
        grads[:, cols(1)] = grad_k
        grads[:, cols(2)] = grad_v
        grads[:, cols(3)] = mixed
        return 0

    lax.fori_loop(0, width // 128, pair, 0)


def where_am_i():
    me = lax.axis_index("lon")
    return me, me // 4, me // 2 % 2, me % 2


def index_of(z, y, c):
    return (z * 2 + y) * 2 + c


def signal(barrier, **where):
    pl.semaphore_signal(barrier, inc=1, device_id=where, device_id_type=MESH)


def line_neighbours(z, last):
    return (z + last) // (last + 1) + (2 * last - z) // (last + 1)


def gather_kernel(n, shard, fields, full, east, local_sem, send_sem, recv_sem, halo_s, halo_r):
    me, z, y, c = where_am_i()
    x = lax.axis_index("grp")
    last = n // 4 - 1
    barrier = pltpu.get_barrier_semaphore()
    signal(barrier, grp=1 - x)
    signal(barrier, lon=index_of(z, y, 1 - c))
    signal(barrier, lon=index_of(z, 1 - y, c))
    signal(barrier, lon=(me + 2 * c - 1 + n) % n)
    pl.when(z > 0)(lambda: signal(barrier, lon=me - 4))
    pl.when(z < last)(lambda: signal(barrier, lon=me + 4))
    pl.semaphore_wait(barrier, 4 + line_neighbours(z, last))
    halo = pltpu.make_async_remote_copy(
        fields, east, halo_s, halo_r, device_id={"lon": (me + n - 1) % n}, device_id_type=MESH)

    def whole(j, way, where, src=None):
        return pltpu.make_async_remote_copy(
            full.at[j] if src is None else src, full.at[j],
            send_sem.at[j, way, 0], recv_sem.at[j, 0], device_id=where, device_id_type=MESH)

    def half(j, h, way, where, src=None):
        return pltpu.make_async_remote_copy(
            full.at[j, h] if src is None else src, full.at[j, h],
            send_sem.at[j, way, h], recv_sem.at[j, h], device_id=where, device_id_type=MESH)

    partner = {"lon": index_of(z, y, 1 - c)}
    across = {"lon": index_of(z, 1 - y, c)}
    right, left, peer = {"lon": me + 4}, {"lon": me - 4}, {"grp": 1 - x}

    def spread(j, act, src=None, to_right=True, to_left=True):
        if to_right:
            pl.when(z < last)(lambda: act(whole(j, 0, right, src)))
        if to_left:
            pl.when(z > 0)(lambda: act(whole(j, 1, left, src)))
        act(half(j, x, 2, across, None if src is None else src.at[x]))
        act(whole(j, 3, partner, src))

    def own_column(t, act):
        def from_left():
            act(me - 4 * t, dict(to_left=False))
        def from_right():
            act(me + 4 * t, dict(to_right=False))
        pl.when(z - t >= 0)(from_left)
        pl.when(z + t <= last)(from_right)

    def other_column(t, act):
        base = index_of(z, 1 - y, c)
        if t == 0:
            act(base)
        else:
            pl.when(z - t >= 0)(lambda: act(base - 4 * t))
            pl.when(z + t <= last)(lambda: act(base + 4 * t))

    start = lambda copy: copy.start()
    keep = pltpu.make_async_copy(shard, full.at[me], local_sem)
    spread(me, start, shard)
    keep.start()
    halo.start()

    def arrived(j, ways):
        whole(j, 0, right).wait_recv()
        spread(j, start, **ways)

    def across_arrived(j):
        half(j, x, 2, across).wait_recv()
        half(j, x, 4, peer).start()
        half(j, x, 3, partner).start()

    def peer_arrived(j):
        half(j, 1 - x, 4, peer).wait_recv()
        half(j, 1 - x, 3, partner).start()

    for t in range(1, last + 1):
        own_column(t, arrived)
        other_column(t - 1, across_arrived)
        if t > 1:
            other_column(t - 2, peer_arrived)
    other_column(last, across_arrived)
    other_column(last - 1, peer_arrived)
    other_column(last, peer_arrived)

    def partner_block(i, _):
        whole(index_of(i, y, 1 - c), 3, partner).wait_recv()
        half(index_of(i, 1 - y, 1 - c), 0, 3, partner).wait_recv()
        half(index_of(i, 1 - y, 1 - c), 1, 3, partner).wait_recv()
        return 0

    lax.fori_loop(0, last + 1, partner_block, 0)
    keep.wait()
    halo.wait()
    sent = lambda copy: copy.wait_send()
    spread(me, sent, shard)
    for t in range(1, last + 1):
        own_column(t, lambda j, ways: spread(j, sent, **ways))

    def other_sent(j):
        half(j, x, 4, peer).wait_send()
        half(j, x, 3, partner).wait_send()
        half(j, 1 - x, 3, partner).wait_send()

    for t in range(last + 1):
        other_column(t, other_sent)


def scatter_kernel(width, n, p_own, p_east, grads, rolled_t, w_hbm, back, out,
                   w, blocks, from_core, from_y, from_z, keep, send, west,
                   load_sem, core_s, core_r, y_s, y_r, z_s, z_r, west_s, west_r):
    me, z, y, c = where_am_i()
    model = w.shape[0]
    depth = model // n
    last = n // 4 - 1
    load = pltpu.make_async_copy(w_hbm, w, load_sem)
    load.start()
    ahead = (me + 1) % n
    barrier = pltpu.get_barrier_semaphore()
    signal(barrier, lon=index_of(z, y, 1 - c))
    signal(barrier, lon=index_of(z, 1 - y, c))
    signal(barrier, lon=(me + 2 * c - 1 + n) % n)
    pl.when(z > 0)(lambda: signal(barrier, lon=me - 4))
    pl.when(z < last)(lambda: signal(barrier, lon=me + 4))
    pl.semaphore_wait(barrier, 3 + line_neighbours(z, last))

    def remote(src, dst, ssem, rsem, lon):
        return pltpu.make_async_remote_copy(
            src, dst, ssem, rsem, device_id={"lon": lon}, device_id_type=MESH)

    mine = lambda k: blocks.at[k, c]

    def core_copy(k):
        return remote(blocks.at[k, 1 - c], from_core.at[k], core_s.at[k], core_r.at[k], index_of(z, y, 1 - c))

    def y_copy(k):
        return remote(mine(k), from_y.at[k], y_s.at[k], y_r.at[k], index_of(z, 1 - y, c))

    def z_copy(m, d, way):
        to = me + 4 if way == 0 else me - 4
        return remote(mine(4 + m), from_z.at[way, d], z_s.at[way, m], z_r.at[way, d], to)

    def weight_block(chip, k):
        rows = pl.ds(pl.multiple_of(chip * 2 * depth, 2 * depth), 2 * depth)
        for part, begin, end in ((0, 0, 3 * width), (1, 3 * width, 4 * width)):
            def chunk(t, _):
                cols = pl.ds(pl.multiple_of(t * 256, 256), 256)
                both = dot(rolled_t[part, rows, :], grads[:, cols], ((1,), (0,))).astype(bf16)
                blocks[k, 0, :, cols] = both[:depth]
                blocks[k, 1, :, cols] = both[depth:]
                return 0
            lax.fori_loop(begin // 256, end // 256, chunk, 0)

    order = [3 - 3 * (z // 2), (2 + 3 * z) % 5, 1 + z % 2, z]

    def add(dst, *others):
        total = dst[...].astype(f32)
        for other in others:
            total += other[...].astype(f32)
        dst[...] = total.astype(bf16)

    def pass_across(k):
        core_copy(k).wait_recv()
        add(mine(k), from_core.at[k])
        y_copy(k).start()

    def block_step(k):
        chip = order[k % 4] * 2 + (1 - y if k < 4 else y)
        weight_block(chip, k)
        core_copy(k).start()
        if 1 <= k <= 4:
            pass_across(k - 1)

    def project(t, _):
        rows = pl.ds(pl.multiple_of(t * 256, 256), 256)
        attended = dot(grads[:, 3 * width :], w[rows, 3 * width :], ((1,), (1,))).astype(bf16)
        grad_normed = dot(grads[:, : 3 * width], w[rows, : 3 * width], ((1,), (1,))).astype(bf16)
        for part, field in enumerate((attended, grad_normed)):
            keep[part, :, rows] = dot(p_own[...], field, ((0,), (0,))).astype(bf16)
            send[part, :, rows] = dot(p_east[...], field, ((0,), (0,))).astype(bf16)
        return 0

    west_copy = remote(send, west, west_s, west_r, ahead)

    def project_all():
        load.wait()
        lax.fori_loop(0, model // 256, project, 0)
        west_copy.start()

    inner = (z + 1) // 2 % 2

    def line_step(m):
        d = order[m]
        core_copy(4 + m).wait_recv()
        y_copy(m).wait_recv()
        add(mine(4 + m), from_core.at[4 + m], from_y.at[m])
        if m < 3:
            def go_right():
                def more():
                    z_copy(m, d, 0).wait_recv()
                    add(mine(4 + m), from_z.at[0, d])
                pl.when(z > 0)(more)
                z_copy(m, d, 0).start()

            def go_left():
                def more():
                    z_copy(m, d, 1).wait_recv()
                    add(mine(4 + m), from_z.at[1, d])
                pl.when(z < last)(more)
                z_copy(m, d, 1).start()

            pl.when(d > z)(go_right)
            pl.when(d < z)(go_left)

    for k in range(5):
        block_step(k)
    pl.when(inner == 1)(project_all)
    line_step(0)
    block_step(5)
    pl.when(inner == 0)(project_all)
    line_step(1)
    block_step(6)
    block_step(7)
    line_step(2)
    line_step(3)
    west_copy.wait_recv()
    back[...] = (keep[...].astype(f32) + west[...].astype(f32)).astype(bf16)
    out[...] = blocks[7, c].astype(f32)

    def final(way):
        z_copy(3, z, way).wait_recv()
        out[...] += from_z[way, z].astype(f32)

    pl.when(z > 0)(lambda: final(0))
    pl.when(z < last)(lambda: final(1))
    west_copy.wait_send()
    for k in range(8):
        core_copy(k).wait_send()
    for k in range(4):
        y_copy(k).wait_send()
    for m in range(3):
        d = order[m]
        pl.when(d > z)(lambda: z_copy(m, d, 0).wait_send())
        pl.when(d < z)(lambda: z_copy(m, d, 1).wait_send())


def on_device(tokens, land, surface, gain, weights, shifts, index_table, bias_table, cotangent):
    levels, tile_rows, tile_cols, model = tokens.shape
    heads = bias_table.shape[2]
    entries = bias_table.shape[1]
    width = weights.shape[1] // 4
    count = levels * tile_rows * tile_cols
    area = tile_rows * tile_rows
    lats = lax.axis_size("lat")
    n = lax.axis_size("lon")
    depth = model // n
    dma = pltpu.SemaphoreType.DMA

    surface_term = jnp.where(land[None, :, :, None] == 1, surface[1], surface[0])
    stream = (tokens.astype(f32) + surface_term).astype(bf16)
    fields = jnp.stack([normalize(stream, gain), cotangent])
    row_shift = shifts[:, 0]
    if lats > 1:
        below = passed_along(fields, "lat", -1)
        both = jnp.concatenate([fields, below], axis=2)
        fields = jax.vmap(lambda f: take_levels(f[None], row_shift, 2, tile_rows)[0])(both)
        row_shift = jnp.zeros_like(row_shift)
    mine = fields.reshape(2, count, model)
    w, east = pl.pallas_call(
        functools.partial(gather_kernel, n),
        name="gather",
        out_shape=(
            jax.ShapeDtypeStruct((n, 2, depth // 2, 4 * width), bf16),
            jax.ShapeDtypeStruct((2, count, model), bf16),
        ),
        in_specs=[VMEM, VMEM],
        out_specs=(ANY, ANY),
        scratch_shapes=[dma, dma((n, 5, 2)), dma((n, 2)), dma, dma],
        compiler_params=pltpu.CompilerParams(
            collective_id=0, has_side_effects=True, vmem_limit_bytes=60 * 2**20
        ),
        cost_estimate=pl.CostEstimate(flops=0, bytes_accessed=120 * 10**6, transcendentals=0),
    )(weights.reshape(2, depth // 2, 4 * width), mine)
    w = w.reshape(model, 4 * width)

    cell = jnp.arange(count, dtype=jnp.int32)
    lev, row, col = cell // (tile_rows * tile_cols), cell // tile_cols % tile_rows, cell % tile_cols
    from_row = (row + row_shift[lev]) % tile_rows
    from_col = col + shifts[lev, 1]
    source = lev * tile_rows * tile_cols + from_row * tile_cols + from_col % tile_cols
    hit = source[:, None] == cell[None, :]
    inside = (from_col < tile_cols)[:, None]
    p_own = jnp.where(hit & inside, 1.0, 0.0).astype(bf16)
    p_east = jnp.where(hit & ~inside, 1.0, 0.0).astype(bf16)

    onehot = (index_table[:, :, None] == jnp.arange(entries, dtype=jnp.int32)).astype(f32)
    bias = jnp.einsum("qkr,lrh->hlqk", onehot, bias_table, precision=lax.Precision.HIGHEST)
    total_rows = tile_rows * lats
    row_number = lax.axis_index("lat") * tile_rows + jnp.arange(tile_rows, dtype=jnp.int32)
    group = row_number[None, :] >= (total_rows - shifts[:, 0])[:, None]
    group = jnp.repeat(group, tile_rows, axis=1)
    allowed = group[:, :, None] == group[:, None, :]
    bias = jnp.where(allowed[None], bias, -1e30)
    other = jnp.full((heads, area, area), -jnp.inf, f32)
    bias = jnp.concatenate(
        [jnp.concatenate([bias[:, 0], other], axis=2), jnp.concatenate([other, bias[:, 1]], axis=2)],
        axis=1,
    )

    params = pltpu.CompilerParams(vmem_limit_bytes=56 * 2**20)
    grads, rolled_t = pl.pallas_call(
        functools.partial(attend_kernel, width),
        name="attend",
        out_shape=(
            jax.ShapeDtypeStruct((count, 4 * width), bf16),
            jax.ShapeDtypeStruct((2, model, count), bf16),
        ),
        in_specs=[VMEM] * 6,
        out_specs=(VMEM, VMEM),
        scratch_shapes=[pltpu.VMEM((2, count, model), bf16), pltpu.VMEM((count, 4 * width), bf16)],
        compiler_params=params,
        cost_estimate=pl.CostEstimate(flops=3 * 10**9, bytes_accessed=15 * 10**6, transcendentals=200000),
    )(p_own, p_east, mine, east, w, bias)
    block = (depth, 4 * width)
    back, summed = pl.pallas_call(
        functools.partial(scatter_kernel, width, n),
        name="scatter",
        out_shape=(
            jax.ShapeDtypeStruct((2, count, model), bf16),
            jax.ShapeDtypeStruct(block, f32),
        ),
        in_specs=[VMEM] * 4 + [ANY],
        out_specs=(VMEM, VMEM),
        scratch_shapes=[
            pltpu.VMEM((model, 4 * width), bf16),
            pltpu.VMEM((8, 2) + block, bf16),
            pltpu.VMEM((8,) + block, bf16),
            pltpu.VMEM((4,) + block, bf16),
            pltpu.VMEM((2, 4) + block, bf16),
            pltpu.VMEM((2, count, model), bf16),
            pltpu.VMEM((2, count, model), bf16),
            pltpu.VMEM((2, count, model), bf16),
            dma, dma((8,)), dma((8,)), dma((4,)), dma((4,)), dma((2, 4)), dma((2, 4)), dma, dma,
        ],
        compiler_params=pltpu.CompilerParams(
            collective_id=1, has_side_effects=True, vmem_limit_bytes=60 * 2**20
        ),
        cost_estimate=pl.CostEstimate(flops=3 * 10**9, bytes_accessed=150 * 10**6, transcendentals=0),
    )(p_own, p_east, grads, rolled_t, w)
    back = back.reshape(2, levels, tile_rows, tile_cols, model)
    if lats > 1:
        above = passed_along(back, "lat", 1)
        both = jnp.concatenate([above, back], axis=2)
        starts = tile_rows - shifts[:, 0]
        back = jax.vmap(lambda f: take_levels(f[None], starts, 2, tile_rows)[0])(both)
    output = (stream.astype(f32) + back[0].astype(f32)).astype(bf16)
    grad_stream = normalize_back(stream, gain, back[1])
    grad_tokens = (cotangent.astype(f32) + grad_stream).astype(bf16)
    if lats > 1:
        summed = lax.psum(summed, "lat")
    token_count = count * lats * lax.axis_size("lon")
    grad_weights = summed * (1.0 / math.sqrt(token_count))
    return (output, grad_tokens, grad_weights)


def solution(mesh):
    return jax.shard_map(
        on_device,
        mesh=mesh,
        in_specs=(
            P("grp", "lat", "lon", None),
            P(("grp", "lat"), "lon"),
            P(),
            P(),
            P("lon", None),
            P(),
            P(),
            P("lat", None, None),
            P("grp", "lat", "lon", None),
        ),
        out_specs=(
            P("grp", "lat", "lon", None),
            P("grp", "lat", "lon", None),
            P(("grp", "lon"), None),
        ),
        check_vma=False,
    )
```

```python
import functools
import math

import jax
import jax.numpy as jnp
from jax import lax
from jax.experimental import pallas as pl
from jax.experimental.pallas import tpu as pltpu
from jax.sharding import PartitionSpec as P

epsilon = 1e-05
f32 = jnp.float32
bf16 = jnp.bfloat16
MESH = pl.DeviceIdType.MESH
ANY = pl.BlockSpec(memory_space=pl.ANY)
VMEM = pl.BlockSpec(memory_space=pltpu.VMEM)


def passed_along(shard, axis, by):
    count = lax.axis_size(axis)
    return lax.ppermute(shard, axis, [(i, (i + by) % count) for i in range(count)])


def dot(a, b, dims):
    return lax.dot_general(a, b, ((dims[0], dims[1]), ((), ())), preferred_element_type=f32)


def normalize(stream, gain):
    values = stream.astype(f32)
    center = values - jnp.mean(values, axis=-1, keepdims=True)
    spread = lax.rsqrt(jnp.mean(center * center, axis=-1, keepdims=True) + epsilon)
    return (center * spread * gain).astype(bf16)


def normalize_back(stream, gain, grad_normed):
    values = stream.astype(f32)
    center = values - jnp.mean(values, axis=-1, keepdims=True)
    spread = lax.rsqrt(jnp.mean(center * center, axis=-1, keepdims=True) + epsilon)
    scaled = center * spread
    upstream = grad_normed.astype(f32) * gain
    return spread * (
        upstream
        - jnp.mean(upstream, axis=-1, keepdims=True)
        - scaled * jnp.mean(upstream * scaled, axis=-1, keepdims=True)
    )


def take_levels(field, starts, axis, length):

    def one_level(plane, start):
        return lax.dynamic_slice_in_dim(plane, start, length, axis - 1)

    return jax.vmap(one_level, in_axes=(1, 0), out_axes=1)(field, starts)


def attend_kernel(width, p_own, p_east, mine, east, w, bias, grads, rolled_t, rolled, proj):
    tokens, model = rolled.shape[1:]
    for part in range(2):
        def roll_tile(t, _):
            cols = pl.ds(pl.multiple_of(t * 512, 512), 512)
            moved = dot(p_own[...], mine[part, :, cols], ((1,), (0,)))
            moved += dot(p_east[...], east[part, :, cols], ((1,), (0,)))
            rolled[part, :, cols] = moved.astype(bf16)
            rolled_t[part, cols, :] = moved.T.astype(bf16)
            return 0
        lax.fori_loop(0, model // 512, roll_tile, 0)

    def proj_tile(src):
        def body(t, _):
            cols = pl.ds(pl.multiple_of(t * 256, 256), 256)
            proj[:, cols] = dot(rolled[src], w[:, cols], ((1,), (0,))).astype(bf16)
            return 0
        return body

    lax.fori_loop(0, 3 * width // 256, proj_tile(0), 0)
    lax.fori_loop(3 * width // 256, 4 * width // 256, proj_tile(1), 0)

    left = lax.broadcasted_iota(jnp.int32, (tokens, 128), 1) < 64
    scale = 0.125

    def pair(j, _):
        def cols(block):
            return pl.ds(pl.multiple_of(block * width + j * 128, 128), 128)
        q, k, v, g = (proj[:, cols(b)] for b in range(4))
        outs = []
        for half in range(2):
            keep = left if half == 0 else jnp.logical_not(left)
            zero = jnp.zeros_like(q)
            s = dot(jnp.where(keep, q, zero), k, ((1,), (1,))) * scale + bias[2 * j + half]
            top = jnp.max(s, axis=-1, keepdims=True)
            expo = jnp.exp(s - top)
            probs = expo / jnp.sum(expo, axis=-1, keepdims=True)
            probs_b = probs.astype(bf16)
            mixed = dot(probs_b, v, ((1,), (0,)))
            grad_probs = dot(jnp.where(keep, g, zero), v, ((1,), (1,)))
            grad_v = dot(probs_b, g, ((0,), (0,)))
            inner = jnp.sum(probs * grad_probs, axis=-1, keepdims=True)
            gs = (probs * (grad_probs - inner) * scale).astype(bf16)
            outs.append((mixed, dot(gs, k, ((1,), (0,))), dot(gs, q, ((0,), (0,))), grad_v))
        mixed, grad_q, grad_k, grad_v = (jnp.where(left, a, b).astype(bf16) for a, b in zip(*outs))
        grads[:, cols(0)] = grad_q
        grads[:, cols(1)] = grad_k
        grads[:, cols(2)] = grad_v
        grads[:, cols(3)] = mixed
        return 0

    lax.fori_loop(0, width // 128, pair, 0)


def where_am_i():
    me = lax.axis_index("lon")
    return me, me // 4, me // 2 % 2, me % 2


def index_of(z, y, c):
    return (z * 2 + y) * 2 + c


def signal(barrier, **where):
    pl.semaphore_signal(barrier, inc=1, device_id=where, device_id_type=MESH)


def line_neighbours(z, last):
    return (z + last) // (last + 1) + (2 * last - z) // (last + 1)


def gather_kernel(n, shard, fields, full, east, local_sem, send_sem, recv_sem, halo_s, halo_r):
    me, z, y, c = where_am_i()
    x = lax.axis_index("grp")
    last = n // 4 - 1
    barrier = pltpu.get_barrier_semaphore()
    signal(barrier, grp=1 - x)
    signal(barrier, lon=index_of(z, y, 1 - c))
    signal(barrier, lon=index_of(z, 1 - y, c))
    signal(barrier, lon=(me + 2 * c - 1 + n) % n)
    pl.when(z > 0)(lambda: signal(barrier, lon=me - 4))
    pl.when(z < last)(lambda: signal(barrier, lon=me + 4))
    pl.semaphore_wait(barrier, 4 + line_neighbours(z, last))
    halo = pltpu.make_async_remote_copy(
        fields, east, halo_s, halo_r, device_id={"lon": (me + n - 1) % n}, device_id_type=MESH)

    def half(j, h, way, where, src=None):
        return pltpu.make_async_remote_copy(
            full.at[j, h] if src is None else src, full.at[j, h],
            send_sem.at[j, way, h], recv_sem.at[j, h], device_id=where, device_id_type=MESH)

    partner = {"lon": index_of(z, y, 1 - c)}
    across = {"lon": index_of(z, 1 - y, c)}
    right, left, peer = {"lon": me + 4}, {"lon": me - 4}, {"grp": 1 - x}

    halves = ((x, True), (1 - x, False))

    def spread(j, act, h, first, src=None, to_right=True, to_left=True):
        src = None if src is None else src.at[h]
        if to_right:
            pl.when(z < last)(lambda: act(half(j, h, 0, right, src)))
        if to_left:
            pl.when(z > 0)(lambda: act(half(j, h, 1, left, src)))
        if first:
            act(half(j, h, 2, across, src))
        act(half(j, h, 3, partner, src))

    def own_column(t, act):
        def from_left():
            act(me - 4 * t, dict(to_left=False))
        def from_right():
            act(me + 4 * t, dict(to_right=False))
        pl.when(z - t >= 0)(from_left)
        pl.when(z + t <= last)(from_right)

    def other_column(t, act):
        base = index_of(z, 1 - y, c)
        if t == 0:
            act(base)
        else:
            pl.when(z - t >= 0)(lambda: act(base - 4 * t))
            pl.when(z + t <= last)(lambda: act(base + 4 * t))

    start = lambda copy: copy.start()
    keep = pltpu.make_async_copy(shard, full.at[me], local_sem)
    for h, first in halves:
        spread(me, start, h, first, shard)
    keep.start()
    halo.start()

    def arrived(j, ways):
        for h, first in halves:
            half(j, h, 0, right).wait_recv()
            spread(j, start, h, first, **ways)

    def across_arrived(j):
        half(j, x, 2, across).wait_recv()
        half(j, x, 4, peer).start()
        half(j, x, 3, partner).start()

    def peer_arrived(j):
        half(j, 1 - x, 4, peer).wait_recv()
        half(j, 1 - x, 3, partner).start()

    for t in range(1, last + 1):
        own_column(t, arrived)
        other_column(t - 1, across_arrived)
        if t > 1:
            other_column(t - 2, peer_arrived)
    other_column(last, across_arrived)
    other_column(last - 1, peer_arrived)
    other_column(last, peer_arrived)

    def partner_block(i, _):
        for h in range(2):
            half(index_of(i, y, 1 - c), h, 3, partner).wait_recv()
            half(index_of(i, 1 - y, 1 - c), h, 3, partner).wait_recv()
        return 0

    lax.fori_loop(0, last + 1, partner_block, 0)
    keep.wait()
    halo.wait()
    sent = lambda copy: copy.wait_send()
    for h, first in halves:
        spread(me, sent, h, first, shard)
        for t in range(1, last + 1):
            own_column(t, lambda j, ways: spread(j, sent, h, first, **ways))

    def other_sent(j):
        half(j, x, 4, peer).wait_send()
        half(j, x, 3, partner).wait_send()
        half(j, 1 - x, 3, partner).wait_send()

    for t in range(last + 1):
        other_column(t, other_sent)


def scatter_kernel(width, n, p_own, p_east, grads, rolled_t, w_hbm, back, out,
                   w, blocks, from_core, from_y, from_z, keep, send, west,
                   load_sem, core_s, core_r, y_s, y_r, z_s, z_r, west_s, west_r):
    me, z, y, c = where_am_i()
    model = w.shape[0]
    depth = model // n
    last = n // 4 - 1
    load = pltpu.make_async_copy(w_hbm, w, load_sem)
    load.start()
    ahead = (me + 1) % n
    barrier = pltpu.get_barrier_semaphore()
    signal(barrier, lon=index_of(z, y, 1 - c))
    signal(barrier, lon=index_of(z, 1 - y, c))
    signal(barrier, lon=(me + 2 * c - 1 + n) % n)
    pl.when(z > 0)(lambda: signal(barrier, lon=me - 4))
    pl.when(z < last)(lambda: signal(barrier, lon=me + 4))
    pl.semaphore_wait(barrier, 3 + line_neighbours(z, last))

    def remote(src, dst, ssem, rsem, lon):
        return pltpu.make_async_remote_copy(
            src, dst, ssem, rsem, device_id={"lon": lon}, device_id_type=MESH)

    mine = lambda k: blocks.at[k, c]

    def core_copy(k):
        return remote(blocks.at[k, 1 - c], from_core.at[k], core_s.at[k], core_r.at[k], index_of(z, y, 1 - c))

    def y_copy(k):
        return remote(mine(k), from_y.at[k], y_s.at[k], y_r.at[k], index_of(z, 1 - y, c))

    def z_copy(m, d, way):
        to = me + 4 if way == 0 else me - 4
        return remote(mine(4 + m), from_z.at[way, d], z_s.at[way, m], z_r.at[way, d], to)

    def weight_block(chip, k):
        rows = pl.ds(pl.multiple_of(chip * 2 * depth, 2 * depth), 2 * depth)
        for part, begin, end in ((0, 0, 3 * width), (1, 3 * width, 4 * width)):
            def chunk(t, _):
                cols = pl.ds(pl.multiple_of(t * 256, 256), 256)
                both = dot(rolled_t[part, rows, :], grads[:, cols], ((1,), (0,))).astype(bf16)
                blocks[k, 0, :, cols] = both[:depth]
                blocks[k, 1, :, cols] = both[depth:]
                return 0
            lax.fori_loop(begin // 256, end // 256, chunk, 0)

    order = [3 - 3 * (z // 2), (2 + 3 * z) % 5, 1 + z % 2, z]

    def add(dst, *others):
        total = dst[...].astype(f32)
        for other in others:
            total += other[...].astype(f32)
        dst[...] = total.astype(bf16)

    def pass_across(k):
        core_copy(k).wait_recv()
        add(mine(k), from_core.at[k])
        y_copy(k).start()

    def block_step(k):
        chip = order[k % 4] * 2 + (1 - y if k < 4 else y)
        weight_block(chip, k)
        core_copy(k).start()
        if 1 <= k <= 4:
            pass_across(k - 1)

    def project(t, _):
        rows = pl.ds(pl.multiple_of(t * 256, 256), 256)
        attended = dot(grads[:, 3 * width :], w[rows, 3 * width :], ((1,), (1,))).astype(bf16)
        grad_normed = dot(grads[:, : 3 * width], w[rows, : 3 * width], ((1,), (1,))).astype(bf16)
        for part, field in enumerate((attended, grad_normed)):
            keep[part, :, rows] = dot(p_own[...], field, ((0,), (0,))).astype(bf16)
            send[part, :, rows] = dot(p_east[...], field, ((0,), (0,))).astype(bf16)
        return 0

    west_copy = remote(send, west, west_s, west_r, ahead)

    def project_all():
        load.wait()
        lax.fori_loop(0, model // 256, project, 0)
        west_copy.start()

    inner = (z + 1) // 2 % 2

    def line_step(m):
        d = order[m]
        core_copy(4 + m).wait_recv()
        y_copy(m).wait_recv()
        add(mine(4 + m), from_core.at[4 + m], from_y.at[m])
        if m < 3:
            def go_right():
                def more():
                    z_copy(m, d, 0).wait_recv()
                    add(mine(4 + m), from_z.at[0, d])
                pl.when(z > 0)(more)
                z_copy(m, d, 0).start()

            def go_left():
                def more():
                    z_copy(m, d, 1).wait_recv()
                    add(mine(4 + m), from_z.at[1, d])
                pl.when(z < last)(more)
                z_copy(m, d, 1).start()

            pl.when(d > z)(go_right)
            pl.when(d < z)(go_left)

    for k in range(5):
        block_step(k)
    pl.when(inner == 1)(project_all)
    line_step(0)
    block_step(5)
    pl.when(inner == 0)(project_all)
    line_step(1)
    block_step(6)
    block_step(7)
    line_step(2)
    line_step(3)
    west_copy.wait_recv()
    back[...] = (keep[...].astype(f32) + west[...].astype(f32)).astype(bf16)
    out[...] = blocks[7, c].astype(f32)

    def final(way):
        z_copy(3, z, way).wait_recv()
        out[...] += from_z[way, z].astype(f32)

    pl.when(z > 0)(lambda: final(0))
    pl.when(z < last)(lambda: final(1))
    west_copy.wait_send()
    for k in range(8):
        core_copy(k).wait_send()
    for k in range(4):
        y_copy(k).wait_send()
    for m in range(3):
        d = order[m]
        pl.when(d > z)(lambda: z_copy(m, d, 0).wait_send())
        pl.when(d < z)(lambda: z_copy(m, d, 1).wait_send())


def on_device(tokens, land, surface, gain, weights, shifts, index_table, bias_table, cotangent):
    levels, tile_rows, tile_cols, model = tokens.shape
    heads = bias_table.shape[2]
    entries = bias_table.shape[1]
    width = weights.shape[1] // 4
    count = levels * tile_rows * tile_cols
    area = tile_rows * tile_rows
    lats = lax.axis_size("lat")
    n = lax.axis_size("lon")
    depth = model // n
    dma = pltpu.SemaphoreType.DMA

    surface_term = jnp.where(land[None, :, :, None] == 1, surface[1], surface[0])
    stream = (tokens.astype(f32) + surface_term).astype(bf16)
    fields = jnp.stack([normalize(stream, gain), cotangent])
    row_shift = shifts[:, 0]
    if lats > 1:
        below = passed_along(fields, "lat", -1)
        both = jnp.concatenate([fields, below], axis=2)
        fields = jax.vmap(lambda f: take_levels(f[None], row_shift, 2, tile_rows)[0])(both)
        row_shift = jnp.zeros_like(row_shift)
    mine = fields.reshape(2, count, model)
    w, east = pl.pallas_call(
        functools.partial(gather_kernel, n),
        name="gather",
        out_shape=(
            jax.ShapeDtypeStruct((n, 2, depth // 2, 4 * width), bf16),
            jax.ShapeDtypeStruct((2, count, model), bf16),
        ),
        in_specs=[VMEM, VMEM],
        out_specs=(ANY, ANY),
        scratch_shapes=[dma, dma((n, 5, 2)), dma((n, 2)), dma, dma],
        compiler_params=pltpu.CompilerParams(
            collective_id=0, has_side_effects=True, vmem_limit_bytes=60 * 2**20
        ),
        cost_estimate=pl.CostEstimate(flops=0, bytes_accessed=120 * 10**6, transcendentals=0),
    )(weights.reshape(2, depth // 2, 4 * width), mine)
    w = w.reshape(model, 4 * width)

    cell = jnp.arange(count, dtype=jnp.int32)
    lev, row, col = cell // (tile_rows * tile_cols), cell // tile_cols % tile_rows, cell % tile_cols
    from_row = (row + row_shift[lev]) % tile_rows
    from_col = col + shifts[lev, 1]
    source = lev * tile_rows * tile_cols + from_row * tile_cols + from_col % tile_cols
    hit = source[:, None] == cell[None, :]
    inside = (from_col < tile_cols)[:, None]
    p_own = jnp.where(hit & inside, 1.0, 0.0).astype(bf16)
    p_east = jnp.where(hit & ~inside, 1.0, 0.0).astype(bf16)

    onehot = (index_table[:, :, None] == jnp.arange(entries, dtype=jnp.int32)).astype(f32)
    bias = jnp.einsum("qkr,lrh->hlqk", onehot, bias_table, precision=lax.Precision.HIGHEST)
    total_rows = tile_rows * lats
    row_number = lax.axis_index("lat") * tile_rows + jnp.arange(tile_rows, dtype=jnp.int32)
    group = row_number[None, :] >= (total_rows - shifts[:, 0])[:, None]
    group = jnp.repeat(group, tile_rows, axis=1)
    allowed = group[:, :, None] == group[:, None, :]
    bias = jnp.where(allowed[None], bias, -1e30)
    other = jnp.full((heads, area, area), -jnp.inf, f32)
    bias = jnp.concatenate(
        [jnp.concatenate([bias[:, 0], other], axis=2), jnp.concatenate([other, bias[:, 1]], axis=2)],
        axis=1,
    )

    params = pltpu.CompilerParams(vmem_limit_bytes=56 * 2**20)
    grads, rolled_t = pl.pallas_call(
        functools.partial(attend_kernel, width),
        name="attend",
        out_shape=(
            jax.ShapeDtypeStruct((count, 4 * width), bf16),
            jax.ShapeDtypeStruct((2, model, count), bf16),
        ),
        in_specs=[VMEM] * 6,
        out_specs=(VMEM, VMEM),
        scratch_shapes=[pltpu.VMEM((2, count, model), bf16), pltpu.VMEM((count, 4 * width), bf16)],
        compiler_params=params,
        cost_estimate=pl.CostEstimate(flops=3 * 10**9, bytes_accessed=15 * 10**6, transcendentals=200000),
    )(p_own, p_east, mine, east, w, bias)
    block = (depth, 4 * width)
    back, summed = pl.pallas_call(
        functools.partial(scatter_kernel, width, n),
        name="scatter",
        out_shape=(
            jax.ShapeDtypeStruct((2, count, model), bf16),
            jax.ShapeDtypeStruct(block, f32),
        ),
        in_specs=[VMEM] * 4 + [ANY],
        out_specs=(VMEM, VMEM),
        scratch_shapes=[
            pltpu.VMEM((model, 4 * width), bf16),
            pltpu.VMEM((8, 2) + block, bf16),
            pltpu.VMEM((8,) + block, bf16),
            pltpu.VMEM((4,) + block, bf16),
            pltpu.VMEM((2, 4) + block, bf16),
            pltpu.VMEM((2, count, model), bf16),
            pltpu.VMEM((2, count, model), bf16),
            pltpu.VMEM((2, count, model), bf16),
            dma, dma((8,)), dma((8,)), dma((4,)), dma((4,)), dma((2, 4)), dma((2, 4)), dma, dma,
        ],
        compiler_params=pltpu.CompilerParams(
            collective_id=1, has_side_effects=True, vmem_limit_bytes=60 * 2**20
        ),
        cost_estimate=pl.CostEstimate(flops=3 * 10**9, bytes_accessed=150 * 10**6, transcendentals=0),
    )(p_own, p_east, grads, rolled_t, w)
    back = back.reshape(2, levels, tile_rows, tile_cols, model)
    if lats > 1:
        above = passed_along(back, "lat", 1)
        both = jnp.concatenate([above, back], axis=2)
        starts = tile_rows - shifts[:, 0]
        back = jax.vmap(lambda f: take_levels(f[None], starts, 2, tile_rows)[0])(both)
    output = (stream.astype(f32) + back[0].astype(f32)).astype(bf16)
    grad_stream = normalize_back(stream, gain, back[1])
    grad_tokens = (cotangent.astype(f32) + grad_stream).astype(bf16)
    if lats > 1:
        summed = lax.psum(summed, "lat")
    token_count = count * lats * lax.axis_size("lon")
    grad_weights = summed * (1.0 / math.sqrt(token_count))
    return (output, grad_tokens, grad_weights)


def solution(mesh):
    return jax.shard_map(
        on_device,
        mesh=mesh,
        in_specs=(
            P("grp", "lat", "lon", None),
            P(("grp", "lat"), "lon"),
            P(),
            P(),
            P("lon", None),
            P(),
            P(),
            P("lat", None, None),
            P("grp", "lat", "lon", None),
        ),
        out_specs=(
            P("grp", "lat", "lon", None),
            P("grp", "lat", "lon", None),
            P(("grp", "lon"), None),
        ),
        check_vma=False,
    )
```
